512 devices in a mesh: month: 128 (over z, y, core), col: 4 (over x).
Axes of the slice: x: 4, y: 4, z: 16, core: 2. Of those that a mesh axis runs over, the one named last changes fastest.
Arguments:
- even_inverse: bfloat16 [128, 1024, 1024], P('month', None, 'col'), as said below
- odd_diag: bfloat16 [128, 1024, 1024], P('month', None, 'col'), may hold values from -3 to 3
- lower: bfloat16 [128, 2, 1024, 1024], P('month', None, None, 'col'), may hold values from -0.4375 to 0.4375
- arrow: bfloat16 [128, 64, 1024], P('month', None, 'col'), may hold values from -0.09375 to 0.09375
- odd_arrow: bfloat16 [128, 64, 1024], P('month', None, 'col'), may hold values from -0.09375 to 0.09375
- diag_pattern: int32 [128, 8, 8], P('month'), may hold values 0 or 1
- lower_pattern: int32 [128, 2, 8, 8], P('month'), may hold values 0 or 1
- rhs: bfloat16 [128, 1024, 128], P('month', 'col'), may hold values from -6 to 6
- odd_rhs: bfloat16 [128, 1024, 128], P('month', 'col'), may hold values from -6 to 6
- odd_solution: bfloat16 [128, 1024, 128], P('month', 'col'), may hold values from -6 to 6
- fixed_block: float32 [64, 64], replicated, may hold values from -6 to 6
- fixed_load: float32 [64, 128], replicated, may hold values from -6 to 6
- fixed_solution: bfloat16 [64, 128], replicated, may hold values from -6 to 6
Outputs:
- reduced_diag: float32 [128, 1024, 1024], P('month', None, 'col')
- reduced_lower: float32 [128, 1024, 1024], P('month', None, 'col')
- reduced_arrow: float32 [128, 64, 1024], P('month', None, 'col')
- reduced_rhs: float32 [128, 1024, 128], P('month', 'col')
- reduced_fixed: float32 [64, 64], replicated
- fixed_rhs: float32 [64, 128], replicated
- even_solution: float32 [128, 1024, 128], P('month', 'col')
The draws below stay inside these ranges and needn't reach their ends.
Inputs may be any that keep to these rules, and one draw needn't show every extreme that they name: even_inverse[j] is symmetric.
All inputs are finite; a program needn't handle non-finite values. No bound on the sum of `diag_pattern` or of `lower_pattern` on one device may be relied on, other than what follows from the above.
Results may differ from the reference program's by a relative error of at most 0.0029.
Values may be sent and summed in bfloat16 or wider, within the bound.
No kernel may reach another device: no remote copies, remote signals or barrier semaphores. Data moves between devices by JAX's collectives and lax.ppermute only.
A program may use at most 128 MiB of HBM per device.

```python
import jax
import jax.numpy as jnp
from jax import lax

B = 1024
R = 1024
TILE = 128
NT = 8
NR = 8
A = 64
NRHS = 128
PAIRS = 128


def draw_even_inverse(key, part):
    key_off, key_diag = jax.random.split(key)
    noise = jax.random.normal(key_off, (PAIRS, B, B), jnp.float32)
    noise = noise * (0.6 / B ** 0.5)
    symmetric = (noise + jnp.swapaxes(noise, -1, -2)) * 0.5
    diagonal = jnp.exp(jax.random.uniform(key_diag, (PAIRS, B), jnp.float32, 0.0, 0.9))
    identity = jnp.eye(B, dtype=jnp.float32)
    return (symmetric * (1.0 - identity) + identity * diagonal[:, None, :]).astype(jnp.bfloat16)


def set_ends(entries, stream_key, least, high):
    spot = [jax.random.randint(jax.random.fold_in(stream_key, axis), (), 0, length) for axis, length in enumerate(entries.shape)]
    longest = entries.shape.index(max(entries.shape))
    neighbour = spot[:longest] + [(spot[longest] + 1) % entries.shape[longest]] + spot[longest + 1:]
    return entries.at[tuple(spot)].set(least).at[tuple(neighbour)].set(high)


def level_of(stream_key, shape, cuts, smallest, largest):
    def one(dim, shards_of):
        draws = jax.random.uniform(jax.random.fold_in(jax.random.fold_in(stream_key, 6), dim), (shards_of,), jnp.float32, smallest / len(cuts), largest / len(cuts))
        return jnp.repeat(jnp.exp(draws), shape[dim] // shards_of).reshape((-1,) + (1,) * (len(shape) - dim - 1))

    loudness = one(*cuts[0])
    for cut in cuts[1:]:
        loudness = loudness * one(*cut)
    return loudness


def bell_draw(rng, shape, scale, reach, cuts=(), kind=jnp.bfloat16):
    gain = level_of(rng, shape, cuts, -0.22, 0.18) if cuts else 1.0
    entries = jax.random.normal(rng, shape, jnp.float32) * scale * gain
    return jnp.minimum(jnp.maximum(entries, -reach), reach).astype(kind)


def setup_inputs(seed: int = 0) -> dict:
    arg_keys = jax.random.split(jax.random.key(seed), 14)
    even_inverse = draw_even_inverse(jax.random.fold_in(arg_keys[13], 71), 0)
    odd_diag = bell_draw(arg_keys[1], (PAIRS, R, R), 0.5, 3.0, ((0, 128), (2, 4)))
    lower = bell_draw(arg_keys[2], (PAIRS, 2, R, B), (B // 5) ** -0.5, 0.4375, ((0, 128), (3, 4)))
    arrow = bell_draw(arg_keys[3], (PAIRS, A, B), (4 * B) ** -0.5, 0.09375, ((0, 128), (2, 4)))
    odd_arrow = bell_draw(arg_keys[4], (PAIRS, A, R), (4 * B) ** -0.5, 0.09375, ((0, 128), (2, 4)))
    diag_pattern = set_ends((jax.random.randint(arg_keys[5], (PAIRS, NR, NR), 0, 5) < 1).astype(jnp.int32), jax.random.fold_in(arg_keys[5], 1), 0, 1)
    lower_pattern = set_ends((jax.random.randint(arg_keys[6], (PAIRS, 2, NR, NT), 0, 5) < 1).astype(jnp.int32), jax.random.fold_in(arg_keys[6], 1), 0, 1)
    rhs = bell_draw(arg_keys[7], (PAIRS, B, NRHS), 1.0, 6.0, ((0, 128), (1, 4)))
    odd_rhs = bell_draw(arg_keys[8], (PAIRS, R, NRHS), 1.0, 6.0, ((0, 128), (1, 4)))
    odd_solution = bell_draw(arg_keys[9], (PAIRS, R, NRHS), 1.0, 6.0, ((0, 128), (1, 4)))
    fixed_block = bell_draw(arg_keys[10], (A, A), 1.0, 6.0, (), jnp.float32)
    fixed_load = bell_draw(arg_keys[11], (A, NRHS), 1.0, 6.0, (), jnp.float32)
    fixed_solution = bell_draw(arg_keys[12], (A, NRHS), 1.0, 6.0)
    return dict(even_inverse=even_inverse, odd_diag=odd_diag, lower=lower, arrow=arrow, odd_arrow=odd_arrow, diag_pattern=diag_pattern, lower_pattern=lower_pattern, rhs=rhs, odd_rhs=odd_rhs, odd_solution=odd_solution, fixed_block=fixed_block, fixed_load=fixed_load, fixed_solution=fixed_solution)


def tile_mask(pattern):
    return jnp.repeat(jnp.repeat(pattern, TILE, axis=-2), TILE, axis=-1)


def matmul(left, right):
    return jnp.dot(left.astype(jnp.float32), right.astype(jnp.float32), preferred_element_type=jnp.float32)


def reference(even_inverse, odd_diag, lower, arrow, odd_arrow, diag_pattern, lower_pattern, rhs, odd_rhs, odd_solution, fixed_block, fixed_load, fixed_solution):
    prev_solution = jnp.concatenate([jnp.zeros_like(odd_solution[:1]), odd_solution[:-1]], axis=0)

    def per_pair(items):
        index, inverse, low_raw, pat, w_even, b_even, x_odd, x_prev = items
        low_odd = low_raw[1] * tile_mask(pat[1]).astype(low_raw.dtype)
        exists = (index > 0).astype(low_raw.dtype)
        low_prev = low_raw[0] * tile_mask(pat[0]).astype(low_raw.dtype) * exists
        odd_prod = matmul(low_odd, inverse).astype(jnp.bfloat16)
        prev_prod = matmul(low_prev, inverse).astype(jnp.bfloat16)
        arrow_prod = matmul(w_even, inverse).astype(jnp.bfloat16)
        p_term = matmul(low_odd, odd_prod.T)
        q_term = matmul(low_prev, prev_prod.T)
        off_term = -matmul(low_odd, prev_prod.T)
        arrow_here = matmul(w_even, odd_prod.T)
        arrow_next = matmul(w_even, prev_prod.T)
        rhs_here = matmul(odd_prod, b_even)
        rhs_next = matmul(prev_prod, b_even)
        y_even = matmul(inverse.T, b_even)
        fixed_term = matmul(arrow_prod, w_even.T)
        load_term = jnp.dot(w_even.astype(jnp.float32), y_even, precision=lax.Precision.HIGHEST)
        solved = y_even - matmul(prev_prod.T, x_prev) - matmul(odd_prod.T, x_odd) - matmul(arrow_prod.T, fixed_solution)
        return p_term, q_term, off_term, arrow_here, arrow_next, rhs_here, rhs_next, fixed_term, load_term, solved

    indices = jnp.arange(even_inverse.shape[0], dtype=jnp.int32)
    outs = lax.map(per_pair, (indices, even_inverse, lower, lower_pattern, arrow, rhs, odd_solution, prev_solution))
    p_term, q_term, off_term, arrow_here, arrow_next, rhs_here, rhs_next, fixed_term, load_term, solved = outs

    def from_next(values):
        return jnp.concatenate([values[1:], jnp.zeros_like(values[:1])], axis=0)

    diag_mask = tile_mask(diag_pattern).astype(jnp.float32)
    reduced_diag = odd_diag.astype(jnp.float32) * diag_mask - p_term - from_next(q_term)
    reduced_arrow = odd_arrow.astype(jnp.float32) - arrow_here - from_next(arrow_next)
    reduced_rhs = odd_rhs.astype(jnp.float32) - rhs_here - from_next(rhs_next)
    reduced_fixed = fixed_block - jnp.sum(fixed_term, axis=0)
    fixed_rhs = fixed_load - jnp.sum(load_term, axis=0)
    return reduced_diag, off_term, reduced_arrow, reduced_rhs, reduced_fixed, fixed_rhs, solved
```

```python
import jax
import jax.numpy as jnp
from jax import lax
from jax.experimental import pallas as pl
from jax.experimental.pallas import tpu as pltpu
from jax.sharding import Mesh
from jax.sharding import PartitionSpec as P


MONTH = ("month_z", "month_y", "month_k")
BF = jnp.bfloat16
F32 = jnp.float32
T = 128
S = 256
R = 1024
SLOTS = 16
SHARE = SLOTS + 6
CUT = 9
TO_RIGHT = SHARE + 8
TO_LEFT = SHARE + 12
STACK = R + T + 64


def shifted(block, distance):
    n = lax.axis_size(MONTH)
    route = [(i, i + distance) for i in range(n) if 0 <= i + distance < n]
    return lax.ppermute(block, MONTH, route)


def exchanged(pieces, axis):
    return lax.all_to_all(pieces, axis, split_axis=0, concat_axis=0, tiled=True)


def sent_to_all(array, axis):
    return exchanged(jnp.broadcast_to(array, (lax.axis_size(axis), *array.shape)), axis)


def nn(a, b):
    return lax.dot_general(a, b, (((1,), (0,)), ((), ())), preferred_element_type=F32)


def nt(a, b):
    return lax.dot_general(a, b, (((1,), (1,)), ((), ())), preferred_element_type=F32)


def full(shape):
    return pl.BlockSpec(shape, lambda *_: (0,) * len(shape))


def flipped(x):
    return x.astype(F32).T


def call(body, grid, scalars, in_specs, out_specs, out_shape, scratch=()):
    return pl.pallas_call(
        body,
        grid_spec=pltpu.PrefetchScalarGridSpec(
            num_scalar_prefetch=scalars,
            grid=grid,
            in_specs=in_specs,
            out_specs=out_specs,
            scratch_shapes=list(scratch),
        ),
        out_shape=out_shape,
    )


def at_tile(n, count=1):
    return slice(n * T, (n + count) * T)


def pack_body(pos_ref, pat_ref, low_ref, e_ref, b_ref, x_ref, xp_ref, right_ref, left_ref):
    c = pos_ref[0]
    slot = jnp.int32(0)
    for kind in range(2):
        for r in range(8):
            for k in range(2):
                there = pat_ref[kind, r, 2 * c + k] > 0

                @pl.when(there & (slot < SLOTS))
                def _(slot=slot, kind=kind, r=r, k=k):
                    tile = low_ref[0, kind, r * T : (r + 1) * T, k * T : (k + 1) * T]
                    right_ref[pl.ds(pl.multiple_of(slot * T, T), T), :] = tile
                    left_ref[pl.ds(pl.multiple_of((slot + 4) * T, T), T), :] = tile

                slot = slot + there.astype(jnp.int32)
    for n, ref in enumerate((b_ref, x_ref, xp_ref)):
        for k in range(2):
            tile = flipped(ref[0, k * T : (k + 1) * T]).astype(BF)
            right_ref[at_tile(SLOTS + 2 * n + k)] = tile
            left_ref[at_tile(4 + SLOTS + 2 * n + k)] = tile
    for ref, places in (
        (right_ref, ((0, SHARE), (3, SHARE + 4))),
        (left_ref, ((0, 0), (1, SHARE + 4), (2, SHARE + 8))),
    ):
        for off, place in places:
            rows = pl.ds(pl.multiple_of(lax.rem(c + off, 4) * S, S), S)
            for k in range(2):
                ref[at_tile(place + 2 * k, 2)] = e_ref[0, rows, k * T : (k + 1) * T]


def packed(pos, pattern, lower, inverse, rhs, x_odd, x_prev):
    return call(
        pack_body, (1,), 2,
        [full((1, 2, R, S)), full((1, R, S))] + [full((1, S, T))] * 3,
        [full((TO_RIGHT * T, T)), full((TO_LEFT * T, T))],
        (
            jax.ShapeDtypeStruct((TO_RIGHT * T, T), BF),
            jax.ShapeDtypeStruct((TO_LEFT * T, T), BF),
        ),
    )(pos, pattern, lower, inverse, rhs, x_odd, x_prev)


class Shares:
    def __init__(self, pos_ref, own, left, right, far_k0, far_k1, e_ref, wg_ref, far_tiles):
        self.c = pos_ref[0]
        self.refs = {0: (own, 0), 1: (right, 4), 2: (far_tiles, 0), 3: (left, 0)}
        self.left, self.right, self.far_k0, self.far_k1 = left, right, far_k0, far_k1
        self.e_ref, self.wg_ref = e_ref, wg_ref
        far_tiles[at_tile(0, CUT)] = far_k1[at_tile(2, CUT)]
        far_tiles[at_tile(CUT, SHARE - CUT)] = far_k0[at_tile(0, SHARE - CUT)]

    def source(self, r):
        return lax.rem(self.c + r, 4)

    def rows(self, r):
        return pl.ds(pl.multiple_of(self.source(r) * S, S), S)

    def tile(self, r, n):
        ref, first = self.refs[r]
        return ref[pl.ds(pl.multiple_of((n + first) * T, T), T), :]

    def vector(self, r, which):
        ref, first = self.refs[r]
        n = first + SLOTS + 2 * which
        return jnp.concatenate([ref[at_tile(n)], ref[at_tile(n + 1)]], axis=1)

    def weight(self, r):
        return self.wg_ref[self.source(r)]

    def unpack(self, pat_ref, kind, live, stack):
        for r in range(4):
            source = self.source(r)
            slot = jnp.int32(0)
            if kind:
                for i in range(8):
                    for k in range(2):
                        slot = slot + pat_ref[0, i, 2 * source + k]
            for i in range(8):
                for k in range(2):
                    there = pat_ref[kind, i, 2 * source + k] > 0
                    tile = self.tile(r, jnp.minimum(slot, SLOTS - 1))
                    keep = there if live is None else there & (live > 0)
                    cols = slice(r * S + k * T, r * S + (k + 1) * T)
                    stack[i * T : (i + 1) * T, cols] = jnp.where(
                        keep, tile, jnp.zeros_like(tile)
                    )
                    slot = slot + there.astype(jnp.int32)
            stack[R : R + T, r * S : (r + 1) * S] = self.vector(r, 0)
            stack[R + T :, r * S : (r + 1) * S] = self.weight(r)

    def stored(self, r1, r2):
        if r2 == 0:
            return self.e_ref[0, self.rows(r1), :]
        if (r1, r2) == (2, 2):
            halves = [
                self.far_k0[at_tile(SHARE - CUT, 2)],
                self.far_k1[at_tile(0, 2)],
            ]
        else:
            ref, n = {
                (1, 1): (self.right, 0),
                (2, 1): (self.right, 4 + SHARE),
                (3, 1): (self.right, 8 + SHARE),
                (3, 3): (self.left, SHARE),
                (2, 3): (self.left, SHARE + 4),
            }[r1, r2]
            halves = [ref[at_tile(n, 2)], ref[at_tile(n + 2, 2)]]
        return jnp.concatenate(halves, axis=1)

    def times_inverse(self, block, r2):
        total = None
        for r1 in range(4):
            part = block[:, r1 * S : (r1 + 1) * S]
            if r2 == 0 or (r1, r2) in ((1, 1), (2, 1), (3, 1), (2, 2), (2, 3), (3, 3)):
                part = nn(part, self.stored(r1, r2))
            else:
                part = nt(part, self.stored(r2, r1))
            total = part if total is None else total + part
        return total

    def applied(self, which, stack):
        total = None
        for r in range(4):
            part = nn(self.vector(r, which), stack[self.rows(r), :])
            total = part if total is None else total + part
        return total


SHARE_SPECS = [
    full((TO_RIGHT * T, T)), full((TO_RIGHT * T, T)), full((TO_LEFT * T, T)),
    full(((SHARE - CUT + 2) * T, T)), full(((CUT + 2) * T, T)),
    full((1, R, S)), full((4, 64, S)),
]
SHARE_SCRATCH = [pltpu.VMEM((SHARE * T, T), BF), pltpu.VMEM((STACK, R), BF)]


def next_body(pos_ref, pat_ref, *refs):
    ahead_ref, v_ref, z_ref, far_tiles, stack = refs[7:]
    shares = Shares(pos_ref, *refs[:7], far_tiles)
    shares.unpack(pat_ref, 0, pos_ref[1], stack)
    low = stack[shares.rows(0), :]
    for r in range(4):
        v_ref[:, r * S : (r + 1) * S] = shares.times_inverse(low, r).astype(BF)
    ahead_ref[...] = nt(stack[...], v_ref[...]).astype(BF)
    z_ref[...] = shares.applied(2, stack)


def next_terms(pos, pattern, shares, inverse, wg):
    return call(
        next_body, (1,), 2, SHARE_SPECS,
        [full((STACK, S)), full((S, R)), full((T, R))],
        (
            jax.ShapeDtypeStruct((STACK, S), BF),
            jax.ShapeDtypeStruct((S, R), BF),
            jax.ShapeDtypeStruct((T, R), F32),
        ),
        SHARE_SCRATCH,
    )(pos, pattern, *shares, inverse, wg)


def here_body(pos_ref, pat_ref, *refs):
    v_ref, z_ref, f_ref, here_ref, off_ref, solved_ref, far_tiles, stack, u_rows = refs[7:]
    shares = Shares(pos_ref, *refs[:7], far_tiles)
    shares.unpack(pat_ref, 1, None, stack)
    low = stack[shares.rows(0), :]
    for r in range(4):
        u_rows[:, r * S : (r + 1) * S] = shares.times_inverse(low, r).astype(BF)
    here_ref[...] = nt(stack[...], u_rows[...])
    off_ref[0] = -nt(stack[:R], v_ref[...])
    z = z_ref[...] + shares.applied(1, stack)
    fixed = flipped(f_ref[...]).astype(BF)
    z = z + nn(fixed, stack[R + T :])
    rest = stack[R : R + T].astype(F32) - z
    high = rest.astype(BF)
    low_part = (rest - high.astype(F32)).astype(BF)
    total = None
    for r in range(4):
        cols = slice(r * S, (r + 1) * S)
        block = shares.stored(r, 0)
        part = nn(high[:, cols], block) + nn(low_part[:, cols], block)
        total = part if total is None else total + part
    solved_ref[0] = total.T


def here_terms(pos, pattern, shares, inverse, wg, v_rows, z, fixed):
    return call(
        here_body, (1,), 2,
        SHARE_SPECS + [full((S, R)), full((T, R)), full((64, T))],
        [full((STACK, S)), full((1, R, S)), full((1, S, T))],
        (
            jax.ShapeDtypeStruct((STACK, S), F32),
            jax.ShapeDtypeStruct((1, R, S), F32),
            jax.ShapeDtypeStruct((1, S, T), F32),
        ),
        SHARE_SCRATCH + [pltpu.VMEM((S, R), BF)],
    )(pos, pattern, *shares, inverse, wg, v_rows, z, fixed)


def reduced_body(
    pos_ref, dpat_ref, here_ref, got_ref, diag_ref, oarrow_ref, orhs_ref, rd_ref, ra_ref, rr_ref
):
    c = pos_ref[0]
    for i in range(8):
        for k in range(2):
            keep = dpat_ref[i, 2 * c + k] > 0
            rs, cs = slice(i * T, (i + 1) * T), slice(k * T, (k + 1) * T)
            tile = diag_ref[0, rs, cs].astype(F32)
            total = here_ref[rs, cs] + got_ref[rs, cs].astype(F32)
            rd_ref[0, rs, cs] = jnp.where(keep, tile, jnp.zeros_like(tile)) - total
    tail = here_ref[R:] + got_ref[R:].astype(F32)
    rr_ref[0] = orhs_ref[0].astype(F32) - tail[:T].T
    ra_ref[0] = oarrow_ref[0].astype(F32) - tail[T:]


def reduced_terms(pos, dpattern, here, got, diag, oarrow, orhs):
    return call(
        reduced_body, (1,), 2,
        [
            full((STACK, S)), full((STACK, S)), full((1, R, S)),
            full((1, 64, S)), full((1, S, T)),
        ],
        [full((1, R, S)), full((1, 64, S)), full((1, S, T))],
        (
            jax.ShapeDtypeStruct((1, R, S), F32),
            jax.ShapeDtypeStruct((1, 64, S), F32),
            jax.ShapeDtypeStruct((1, S, T), F32),
        ),
    )(pos, dpattern, here, got, diag, oarrow, orhs)


def spread_body(pieces_ref, out_ref):
    total = pieces_ref[0]
    for n in range(1, pieces_ref.shape[0]):
        total = total + pieces_ref[n]
    for n in range(out_ref.shape[0]):
        out_ref[n] = total


def spread(pieces, copies):
    shape = pieces.shape[1:]
    return call(
        spread_body, (1,), 0, [full(pieces.shape)], full((copies, *shape)),
        jax.ShapeDtypeStruct((copies, *shape), F32),
    )(pieces)


def settle_body(pieces_ref, block_ref, load_ref, fixed_ref, rhs_ref, over_ref):
    for n in range(8):
        total = pieces_ref[4 * n]
        for k in range(1, 4):
            total = total + pieces_ref[4 * n + k]
        if n < 4:
            rows = slice(16 * n, 16 * n + 16)
            fixed_ref[rows] = block_ref[rows] - total[:, :64]
        else:
            rows = slice(16 * n - 64, 16 * n - 48)
            rhs_ref[rows] = load_ref[rows] - total
        if n == 0:
            over_ref[...] = total[:8]


def settled(pieces, fixed_block, fixed_load):
    return call(
        settle_body, (1,), 0,
        [full((32, 16, 128)), full((64, 64)), full((64, 128))],
        [full((64, 64)), full((64, 128)), full((8, 128))],
        (
            jax.ShapeDtypeStruct((64, 64), F32),
            jax.ShapeDtypeStruct((64, 128), F32),
            jax.ShapeDtypeStruct((8, 128), F32),
        ),
    )(pieces, fixed_block, fixed_load)


def along_col(block, distance):
    return lax.ppermute(block, "col", [(i, (i + distance) % 4) for i in range(4)])


def fixed_body(pat_ref, wg_ref, e_ref, w_ref, b_ref, sums_ref):
    g32 = nn(wg_ref[0], e_ref[0, :S])
    for k in range(1, 4):
        g32 += nn(wg_ref[k], e_ref[0, k * S : (k + 1) * S])
    sums_ref[:64, :64] = nt(g32.astype(BF), w_ref[0])
    over = jnp.int32(0)
    for c in range(4):
        count = jnp.int32(0)
        for kind in range(2):
            for r in range(8):
                for k in range(2):
                    count = count + pat_ref[kind, r, 2 * c + k]
        over = over + (count > SLOTS).astype(jnp.int32)
    sums_ref[:64, 64:] = jnp.full((64, 64), over.astype(F32))
    sums_ref[64:] = lax.dot_general(
        g32, b_ref[0].astype(F32), (((1,), (0,)), ((), ())),
        precision=lax.Precision.HIGHEST, preferred_element_type=F32,
    )


def fixed_terms(pattern, wg, inverse, arrow, rhs):
    return call(
        fixed_body, (1,), 1,
        [full((4, 64, S)), full((1, R, S)), full((1, 64, S)), full((1, S, T))],
        full((128, 128)),
        jax.ShapeDtypeStruct((128, 128), F32),
    )(pattern, wg, inverse, arrow, rhs)


def tile_mask(pattern):
    return jnp.repeat(jnp.repeat(pattern, T, axis=-2), T, axis=-1)


def gathered(array, dim):
    return jnp.concatenate(list(sent_to_all(array, "col")), axis=dim)


def all_tiles(
    inverse, diag, lower, arrow, oarrow, dpattern, pattern, rhs, orhs, x_odd, fixed
):
    col = lax.axis_index("col")
    exists = (lax.axis_index(MONTH) > 0).astype(BF)
    low_odd = gathered(lower[0, 1], 1) * tile_mask(pattern[1]).astype(BF)
    low_prev = gathered(lower[0, 0], 1) * tile_mask(pattern[0]).astype(BF) * exists
    weight = gathered(arrow[0], 1)
    e = inverse[0]
    odd_cols = nn(low_odd, e).astype(BF)
    prev_cols = nn(low_prev, e).astype(BF)
    arrow_cols = nn(weight, e).astype(BF)
    odd_rows = lax.all_to_all(odd_cols, "col", split_axis=0, concat_axis=1, tiled=True)
    prev_rows = lax.all_to_all(prev_cols, "col", split_axis=0, concat_axis=1, tiled=True)
    loads = gathered(rhs[0], 0)
    odd_full = gathered(x_odd[0], 0)
    got = shifted(
        (nt(low_prev, prev_rows), nt(weight, prev_rows), nn(prev_rows, loads)), -1
    )
    prev_full = shifted(odd_full, 1)
    mask = lax.dynamic_slice_in_dim(tile_mask(dpattern).astype(F32), col * S, S, 1)
    rd = diag[0].astype(F32) * mask - nt(low_odd, odd_rows) - got[0]
    rl = -nt(low_odd, prev_rows)
    ra = oarrow[0].astype(F32) - nt(weight, odd_rows) - got[1]
    rr = orhs[0].astype(F32) - nn(odd_rows, loads) - got[2]

    def tn(a, b):
        return lax.dot_general(a, b, (((0,), (0,)), ((), ())), preferred_element_type=F32)

    solved = (
        tn(e, loads) - tn(prev_cols, prev_full) - tn(odd_cols, odd_full)
        - tn(arrow_cols, fixed)
    )
    return rd[None], rl[None], ra[None], rr[None], solved[None]


def per_device(
    even_inverse, odd_diag, lower, arrow, odd_arrow, diag_pattern, lower_pattern,
    rhs, odd_rhs, odd_solution, fixed_block, fixed_load, fixed_solution,
):
    col = lax.axis_index("col")
    month = lax.axis_index(MONTH)
    pos = jnp.stack([col, (month > 0).astype(jnp.int32)]).astype(jnp.int32)
    pattern, dpattern = lower_pattern[0], diag_pattern[0]

    x_prev = shifted(odd_solution, 1)
    wg = sent_to_all(arrow[0], "col")
    to_right, to_left = packed(
        pos, pattern, lower, even_inverse, rhs, odd_solution, x_prev
    )
    to_right, to_left, wg = lax.optimization_barrier((to_right, to_left, wg))
    left = along_col(to_right, 1)
    right = along_col(to_left, -1)
    far_k0 = along_col(left[CUT * T : (SHARE + 2) * T], 1)
    far_k1 = along_col(right[2 * T : (CUT + 4) * T], -1)
    sums = fixed_terms(pattern, wg, even_inverse, arrow, rhs)
    sums = spread(exchanged(sums.reshape(8, 16, 128), MONTH[1:]), 16)
    sums = spread(exchanged(sums, "month_z"), 32)
    sums = exchanged(sums, (*MONTH[1:], "col"))
    reduced_fixed, fixed_rhs, over = settled(sums, fixed_block, fixed_load)
    shares = (to_right, left, right, far_k0, far_k1)
    ahead, v_rows, z = next_terms(pos, pattern, shares, even_inverse, wg)
    got = shifted(ahead, -1)
    here, off, solved = here_terms(
        pos, pattern, shares, even_inverse, wg, v_rows, z, fixed_solution
    )

    def finish():
        rd, ra, rr = reduced_terms(pos, dpattern, here, got, odd_diag, odd_arrow, odd_rhs)
        return rd, off, ra, rr, solved

    def again():
        return all_tiles(
            even_inverse, odd_diag, lower, arrow, odd_arrow, dpattern, pattern,
            rhs, odd_rhs, odd_solution, fixed_solution,
        )

    rd, rl, ra, rr, solved = lax.cond(over[0, 64] > 0.5, again, finish)
    return rd, rl, ra, rr, reduced_fixed, fixed_rhs, solved


def solution(mesh):
    finer = Mesh(
        mesh.devices.reshape(16, 4, 2, mesh.shape["col"]),
        ("month_z", "month_y", "month_k", "col"),
    )
    cols3, rows3 = P(MONTH, None, "col"), P(MONTH, "col", None)
    return jax.shard_map(
        per_device,
        mesh=finer,
        in_specs=(
            cols3, cols3, P(MONTH, None, None, "col"), cols3, cols3,
            P(MONTH, None, None), P(MONTH, None, None, None),
            rows3, rows3, rows3, P(), P(), P(),
        ),
        out_specs=(cols3, cols3, cols3, rows3, P(), P(), rows3),
        check_vma=False,
    )
```

```python
import jax
import jax.numpy as jnp
from jax import lax
from jax.experimental import pallas as pl
from jax.experimental.pallas import tpu as pltpu
from jax.sharding import Mesh
from jax.sharding import PartitionSpec as P


MONTH = ("month_z", "month_y", "month_k")
BF = jnp.bfloat16
F32 = jnp.float32
T = 128
S = 256
R = 1024
SLOTS = 16
SHARE = SLOTS + 6
CUT = 11
TO_RIGHT = SHARE + 8
TO_LEFT = SHARE + 12
STACK = R + T + 64
VMEM_LIMIT = 20 * 1024 * 1024


def shifted(block, distance):
    n = lax.axis_size(MONTH)
    route = [(i, i + distance) for i in range(n) if 0 <= i + distance < n]
    return lax.ppermute(block, MONTH, route)


def exchanged(pieces, axis):
    return lax.all_to_all(pieces, axis, split_axis=0, concat_axis=0, tiled=True)


def sent_to_all(array, axis):
    return exchanged(jnp.broadcast_to(array, (lax.axis_size(axis), *array.shape)), axis)


def nn(a, b):
    return lax.dot_general(a, b, (((1,), (0,)), ((), ())), preferred_element_type=F32)


def nt(a, b):
    return lax.dot_general(a, b, (((1,), (1,)), ((), ())), preferred_element_type=F32)


def full():
    return pl.BlockSpec(memory_space=pltpu.VMEM)


def flipped(x):
    return x.astype(F32).T


def call(body, grid, scalars, in_specs, out_specs, out_shape, scratch=()):
    return pl.pallas_call(
        body,
        grid_spec=pltpu.PrefetchScalarGridSpec(
            num_scalar_prefetch=scalars,
            grid=grid,
            in_specs=in_specs,
            out_specs=out_specs,
            scratch_shapes=list(scratch),
        ),
        out_shape=out_shape,
        compiler_params=pltpu.CompilerParams(vmem_limit_bytes=VMEM_LIMIT),
    )


def at_tile(n, count=1):
    return slice(n * T, (n + count) * T)


def pack_body(pos_ref, pat_ref, low_ref, e_ref, b_ref, x_ref, xp_ref, right_ref, left_ref):
    c = pos_ref[0]
    slot = jnp.int32(0)
    for kind in range(2):
        for r in range(8):
            for k in range(2):
                there = pat_ref[kind, r, 2 * c + k] > 0

                @pl.when(there & (slot < SLOTS))
                def _(slot=slot, kind=kind, r=r, k=k):
                    tile = low_ref[0, kind, r * T : (r + 1) * T, k * T : (k + 1) * T]
                    right_ref[pl.ds(pl.multiple_of(slot * T, T), T), :] = tile
                    left_ref[pl.ds(pl.multiple_of((slot + 4) * T, T), T), :] = tile

                slot = slot + there.astype(jnp.int32)
    for n, ref in enumerate((b_ref, x_ref, xp_ref)):
        for k in range(2):
            tile = flipped(ref[0, k * T : (k + 1) * T]).astype(BF)
            right_ref[at_tile(SLOTS + 2 * n + k)] = tile
            left_ref[at_tile(4 + SLOTS + 2 * n + k)] = tile
    for ref, places in (
        (right_ref, ((0, SHARE), (3, SHARE + 4))),
        (left_ref, ((0, 0), (1, SHARE + 4), (2, SHARE + 8))),
    ):
        for off, place in places:
            rows = pl.ds(pl.multiple_of(lax.rem(c + off, 4) * S, S), S)
            for k in range(2):
                ref[at_tile(place + 2 * k, 2)] = e_ref[0, rows, k * T : (k + 1) * T]


def packed(pos, pattern, lower, inverse, rhs, x_odd, x_prev):
    return call(
        pack_body, (), 2,
        [full(), full()] + [full()] * 3,
        [full(), full()],
        (
            jax.ShapeDtypeStruct((TO_RIGHT * T, T), BF),
            jax.ShapeDtypeStruct((TO_LEFT * T, T), BF),
        ),
    )(pos, pattern, lower, inverse, rhs, x_odd, x_prev)


class Shares:
    def __init__(self, pos_ref, own, left, right, far_k0, far_k1, e_ref, wg_ref, far_tiles):
        self.c = pos_ref[0]
        self.refs = {0: (own, 0), 1: (right, 4), 2: (far_tiles, 0), 3: (left, 0)}
        self.left, self.right, self.far_k0, self.far_k1 = left, right, far_k0, far_k1
        self.e_ref, self.wg_ref = e_ref, wg_ref
        far_tiles[at_tile(0, CUT)] = far_k1[at_tile(2, CUT)]
        far_tiles[at_tile(CUT, SHARE - CUT)] = far_k0[at_tile(0, SHARE - CUT)]

    def source(self, r):
        return lax.rem(self.c + r, 4)

    def rows(self, r):
        return pl.ds(pl.multiple_of(self.source(r) * S, S), S)

    def tile(self, r, n):
        ref, first = self.refs[r]
        return ref[pl.ds(pl.multiple_of((n + first) * T, T), T), :]

    def vector(self, r, which):
        ref, first = self.refs[r]
        n = first + SLOTS + 2 * which
        return jnp.concatenate([ref[at_tile(n)], ref[at_tile(n + 1)]], axis=1)

    def weight(self, r):
        return self.wg_ref[self.source(r)]

    def unpack(self, pat_ref, kind, live, stack):
        for r in range(4):
            source = self.source(r)
            slot = jnp.int32(0)
            if kind:
                for i in range(8):
                    for k in range(2):
                        slot = slot + pat_ref[0, i, 2 * source + k]
            for i in range(8):
                for k in range(2):
                    there = pat_ref[kind, i, 2 * source + k] > 0
                    tile = self.tile(r, jnp.minimum(slot, SLOTS - 1))
                    keep = there if live is None else there & (live > 0)
                    cols = slice(r * S + k * T, r * S + (k + 1) * T)
                    stack[i * T : (i + 1) * T, cols] = jnp.where(
                        keep, tile, jnp.zeros_like(tile)
                    )
                    slot = slot + there.astype(jnp.int32)
            stack[R : R + T, r * S : (r + 1) * S] = self.vector(r, 0)
            stack[R + T :, r * S : (r + 1) * S] = self.weight(r)

    def stored(self, r1, r2):
        if r2 == 0:
            return self.e_ref[0, self.rows(r1), :]
        if (r1, r2) == (2, 2):
            halves = [
                self.far_k0[at_tile(SHARE - CUT, 2)],
                self.far_k1[at_tile(0, 2)],
            ]
        else:
            ref, n = {
                (1, 1): (self.right, 0),
                (2, 1): (self.right, 4 + SHARE),
                (3, 1): (self.right, 8 + SHARE),
                (3, 3): (self.left, SHARE),
                (2, 3): (self.left, SHARE + 4),
            }[r1, r2]
            halves = [ref[at_tile(n, 2)], ref[at_tile(n + 2, 2)]]
        return jnp.concatenate(halves, axis=1)

    def times_inverse(self, block, r2):
        total = None
        for r1 in range(4):
            part = block[:, r1 * S : (r1 + 1) * S]
            if r2 == 0 or (r1, r2) in ((1, 1), (2, 1), (3, 1), (2, 2), (2, 3), (3, 3)):
                part = nn(part, self.stored(r1, r2))
            else:
                part = nt(part, self.stored(r2, r1))
            total = part if total is None else total + part
        return total

    def applied(self, which, stack):
        total = None
        for r in range(4):
            part = nn(self.vector(r, which), stack[self.rows(r), :])
            total = part if total is None else total + part
        return total


SHARE_SPECS = [
    full(), full(), full(),
    full(), full(),
    full(), full(),
]
SHARE_SCRATCH = [pltpu.VMEM((SHARE * T, T), BF), pltpu.VMEM((STACK, R), BF)]


def next_body(pos_ref, pat_ref, *refs):
    ahead_ref, v_ref, z_ref, far_tiles, stack = refs[7:]
    shares = Shares(pos_ref, *refs[:7], far_tiles)
    shares.unpack(pat_ref, 0, pos_ref[1], stack)
    low = stack[shares.rows(0), :]
    for r in range(4):
        v_ref[:, r * S : (r + 1) * S] = shares.times_inverse(low, r).astype(BF)
    ahead_ref[...] = nt(stack[...], v_ref[...]).astype(BF)
    z_ref[...] = shares.applied(2, stack)


def next_terms(pos, pattern, shares, inverse, wg):
    return call(
        next_body, (), 2, SHARE_SPECS,
        [full(), full(), full()],
        (
            jax.ShapeDtypeStruct((STACK, S), BF),
            jax.ShapeDtypeStruct((S, R), BF),
            jax.ShapeDtypeStruct((T, R), F32),
        ),
        SHARE_SCRATCH,
    )(pos, pattern, *shares, inverse, wg)


def here_body(pos_ref, pat_ref, *refs):
    v_ref, z_ref, f_ref, here_ref, off_ref, solved_ref, far_tiles, stack, u_rows = refs[7:]
    shares = Shares(pos_ref, *refs[:7], far_tiles)
    shares.unpack(pat_ref, 1, None, stack)
    low = stack[shares.rows(0), :]
    for r in range(4):
        u_rows[:, r * S : (r + 1) * S] = shares.times_inverse(low, r).astype(BF)
    here_ref[...] = nt(stack[...], u_rows[...])
    off_ref[0] = -nt(stack[:R], v_ref[...])
    z = z_ref[...] + shares.applied(1, stack)
    fixed = flipped(f_ref[...]).astype(BF)
    z = z + nn(fixed, stack[R + T :])
    rest = stack[R : R + T].astype(F32) - z
    high = rest.astype(BF)
    low_part = (rest - high.astype(F32)).astype(BF)
    total = None
    for r in range(4):
        cols = slice(r * S, (r + 1) * S)
        block = shares.stored(r, 0)
        part = nn(high[:, cols], block) + nn(low_part[:, cols], block)
        total = part if total is None else total + part
    solved_ref[0] = total.T


def here_terms(pos, pattern, shares, inverse, wg, v_rows, z, fixed):
    return call(
        here_body, (), 2,
        SHARE_SPECS + [full(), full(), full()],
        [full(), full(), full()],
        (
            jax.ShapeDtypeStruct((STACK, S), F32),
            jax.ShapeDtypeStruct((1, R, S), F32),
            jax.ShapeDtypeStruct((1, S, T), F32),
        ),
        SHARE_SCRATCH + [pltpu.VMEM((S, R), BF)],
    )(pos, pattern, *shares, inverse, wg, v_rows, z, fixed)


def reduced_body(
    pos_ref, dpat_ref, here_ref, got_ref, diag_ref, oarrow_ref, orhs_ref, rd_ref, ra_ref, rr_ref
):
    c = pos_ref[0]
    for i in range(8):
        for k in range(2):
            keep = dpat_ref[i, 2 * c + k] > 0
            rs, cs = slice(i * T, (i + 1) * T), slice(k * T, (k + 1) * T)
            tile = diag_ref[0, rs, cs].astype(F32)
            total = here_ref[rs, cs] + got_ref[rs, cs].astype(F32)
            rd_ref[0, rs, cs] = jnp.where(keep, tile, jnp.zeros_like(tile)) - total
    tail = here_ref[R:] + got_ref[R:].astype(F32)
    rr_ref[0] = orhs_ref[0].astype(F32) - tail[:T].T
    ra_ref[0] = oarrow_ref[0].astype(F32) - tail[T:]


def reduced_terms(pos, dpattern, here, got, diag, oarrow, orhs):
    return call(
        reduced_body, (), 2,
        [
            full(), full(), full(),
            full(), full(),
        ],
        [full(), full(), full()],
        (
            jax.ShapeDtypeStruct((1, R, S), F32),
            jax.ShapeDtypeStruct((1, 64, S), F32),
            jax.ShapeDtypeStruct((1, S, T), F32),
        ),
    )(pos, dpattern, here, got, diag, oarrow, orhs)


def spread_body(pieces_ref, out_ref):
    total = pieces_ref[0]
    for n in range(1, pieces_ref.shape[0]):
        total = total + pieces_ref[n]
    for n in range(out_ref.shape[0]):
        out_ref[n] = total


def spread(pieces, copies):
    shape = pieces.shape[1:]
    return call(
        spread_body, (), 0, [full()], full(),
        jax.ShapeDtypeStruct((copies, *shape), F32),
    )(pieces)


def settle_body(pieces_ref, block_ref, load_ref, fixed_ref, rhs_ref, over_ref):
    for n in range(8):
        total = pieces_ref[4 * n]
        for k in range(1, 4):
            total = total + pieces_ref[4 * n + k]
        if n < 4:
            rows = slice(16 * n, 16 * n + 16)
            fixed_ref[rows] = block_ref[rows] - total[:, :64]
        else:
            rows = slice(16 * n - 64, 16 * n - 48)
            rhs_ref[rows] = load_ref[rows] - total
        if n == 0:
            over_ref[0, 0] = jnp.max(total[:8, 64:]).astype(jnp.int32)


def settled(pieces, fixed_block, fixed_load):
    return call(
        settle_body, (), 0,
        [full(), full(), full()],
        [
            full(), full(),
            pl.BlockSpec(memory_space=pltpu.SMEM),
        ],
        (
            jax.ShapeDtypeStruct((64, 64), F32),
            jax.ShapeDtypeStruct((64, 128), F32),
            jax.ShapeDtypeStruct((1, 1), jnp.int32),
        ),
    )(pieces, fixed_block, fixed_load)


def along_col(block, distance):
    return lax.ppermute(block, "col", [(i, (i + distance) % 4) for i in range(4)])


def fixed_body(pat_ref, wg_ref, e_ref, w_ref, b_ref, sums_ref):
    g32 = nn(wg_ref[0], e_ref[0, :S])
    for k in range(1, 4):
        g32 += nn(wg_ref[k], e_ref[0, k * S : (k + 1) * S])
    sums_ref[:64, :64] = nt(g32.astype(BF), w_ref[0])
    over = jnp.int32(0)
    for c in range(4):
        count = jnp.int32(0)
        for kind in range(2):
            for r in range(8):
                for k in range(2):
                    count = count + pat_ref[kind, r, 2 * c + k]
        over = over + (count > SLOTS).astype(jnp.int32)
    sums_ref[:64, 64:] = jnp.full((64, 64), over.astype(F32))
    sums_ref[64:] = lax.dot_general(
        g32, b_ref[0].astype(F32), (((1,), (0,)), ((), ())),
        precision=lax.Precision.HIGHEST, preferred_element_type=F32,
    )


def fixed_terms(pattern, wg, inverse, arrow, rhs):
    return call(
        fixed_body, (), 1,
        [full(), full(), full(), full()],
        full(),
        jax.ShapeDtypeStruct((128, 128), F32),
    )(pattern, wg, inverse, arrow, rhs)


def tile_mask(pattern):
    return jnp.repeat(jnp.repeat(pattern, T, axis=-2), T, axis=-1)


def gathered(array, dim):
    return jnp.concatenate(list(sent_to_all(array, "col")), axis=dim)


def all_tiles(
    inverse, diag, lower, arrow, oarrow, dpattern, pattern, rhs, orhs, x_odd, fixed
):
    col = lax.axis_index("col")
    exists = (lax.axis_index(MONTH) > 0).astype(BF)
    low_odd = gathered(lower[0, 1], 1) * tile_mask(pattern[1]).astype(BF)
    low_prev = gathered(lower[0, 0], 1) * tile_mask(pattern[0]).astype(BF) * exists
    weight = gathered(arrow[0], 1)
    e = inverse[0]
    odd_cols = nn(low_odd, e).astype(BF)
    prev_cols = nn(low_prev, e).astype(BF)
    arrow_cols = nn(weight, e).astype(BF)
    odd_rows = lax.all_to_all(odd_cols, "col", split_axis=0, concat_axis=1, tiled=True)
    prev_rows = lax.all_to_all(prev_cols, "col", split_axis=0, concat_axis=1, tiled=True)
    loads = gathered(rhs[0], 0)
    odd_full = gathered(x_odd[0], 0)
    got = shifted(
        (nt(low_prev, prev_rows), nt(weight, prev_rows), nn(prev_rows, loads)), -1
    )
    prev_full = shifted(odd_full, 1)
    mask = lax.dynamic_slice_in_dim(tile_mask(dpattern).astype(F32), col * S, S, 1)
    rd = diag[0].astype(F32) * mask - nt(low_odd, odd_rows) - got[0]
    rl = -nt(low_odd, prev_rows)
    ra = oarrow[0].astype(F32) - nt(weight, odd_rows) - got[1]
    rr = orhs[0].astype(F32) - nn(odd_rows, loads) - got[2]

    def tn(a, b):
        return lax.dot_general(a, b, (((0,), (0,)), ((), ())), preferred_element_type=F32)

    solved = (
        tn(e, loads) - tn(prev_cols, prev_full) - tn(odd_cols, odd_full)
        - tn(arrow_cols, fixed)
    )
    return rd[None], rl[None], ra[None], rr[None], solved[None]


def per_device(
    even_inverse, odd_diag, lower, arrow, odd_arrow, diag_pattern, lower_pattern,
    rhs, odd_rhs, odd_solution, fixed_block, fixed_load, fixed_solution,
):
    col = lax.axis_index("col")
    month = lax.axis_index(MONTH)
    pos = jnp.stack([col, (month > 0).astype(jnp.int32)]).astype(jnp.int32)
    pattern, dpattern = lower_pattern[0], diag_pattern[0]

    x_prev = shifted(odd_solution, 1)
    wg = sent_to_all(arrow[0], "col")
    to_right, to_left = packed(
        pos, pattern, lower, even_inverse, rhs, odd_solution, x_prev
    )
    left = along_col(to_right, 1)
    right = along_col(to_left, -1)
    far_k0 = along_col(left[CUT * T : (SHARE + 2) * T], 1)
    far_k1 = along_col(right[2 * T : (CUT + 4) * T], -1)
    sums = fixed_terms(pattern, wg, even_inverse, arrow, rhs)
    sums = spread(exchanged(sums.reshape(8, 16, 128), MONTH[1:]), 16)
    sums = spread(exchanged(sums, "month_z"), 32)
    sums = exchanged(sums, (*MONTH[1:], "col"))
    reduced_fixed, fixed_rhs, over = settled(sums, fixed_block, fixed_load)
    shares = (to_right, left, right, far_k0, far_k1)
    ahead, v_rows, z = next_terms(pos, pattern, shares, even_inverse, wg)
    got = shifted(ahead, -1)
    here, off, solved = here_terms(
        pos, pattern, shares, even_inverse, wg, v_rows, z, fixed_solution
    )

    def finish():
        rd, ra, rr = reduced_terms(pos, dpattern, here, got, odd_diag, odd_arrow, odd_rhs)
        return rd, off, ra, rr, solved

    def again():
        return all_tiles(
            even_inverse, odd_diag, lower, arrow, odd_arrow, dpattern, pattern,
            rhs, odd_rhs, odd_solution, fixed_solution,
        )

    rd, rl, ra, rr, solved = lax.cond(over[0, 0] > 0, again, finish)
    return rd, rl, ra, rr, reduced_fixed, fixed_rhs, solved


def solution(mesh):
    finer = Mesh(
        mesh.devices.reshape(16, 4, 2, mesh.shape["col"]),
        ("month_z", "month_y", "month_k", "col"),
    )
    cols3, rows3 = P(MONTH, None, "col"), P(MONTH, "col", None)
    return jax.shard_map(
        per_device,
        mesh=finer,
        in_specs=(
            cols3, cols3, P(MONTH, None, None, "col"), cols3, cols3,
            P(MONTH, None, None), P(MONTH, None, None, None),
            rows3, rows3, rows3, P(), P(), P(),
        ),
        out_specs=(cols3, cols3, cols3, rows3, P(), P(), rows3),
        check_vma=False,
    )
```
